32 devices in a mesh: clip: 4 (over z), band: 4 (over x, core), chan: 2 (over y).
Axes of the slice: x: 2, y: 2, z: 4, core: 2. Of those that a mesh axis runs over, the one named last changes fastest.
Arguments:
- frames: bfloat16 [512, 4, 5120], P(None, 'clip', ('band', 'chan')), may hold values from -6 to 6
- weight: bfloat16 [512, 3, 3, 512], P('chan'), may hold values from -0.09375 to 0.09375
- bias: float32 [512], replicated, may hold values from -3 to 3
- cotangent: bfloat16 [512, 4, 5120], P(None, 'clip', ('band', 'chan')), may hold values from -6 to 6
Outputs:
- outputs: bfloat16 [512, 4, 5120], P(None, 'clip', ('band', 'chan'))
- grad_frames: bfloat16 [512, 4, 5120], P(None, 'clip', ('band', 'chan'))
- grad_weight: float32 [512, 3, 3, 512], P('chan')
- grad_bias: float32 [512], P('chan')
The draws below stay inside these ranges and needn't reach their ends.
All inputs are finite; a program needn't handle non-finite values.
Results may differ from the reference program's by a relative error of at most 0.001.
Values may be sent and summed in bfloat16 or wider, within the bound.
A program may use at most 128 MiB of HBM per device.

```python
import math
import jax
import jax.numpy as jnp
from jax import lax

C = 512
W = 160
H = 32
FRAMES = 4


def block_scale(stream_key, dims, cuts, smallest, top_value):
    gain = 1.0
    for dim, parts in cuts:
        steps = jax.random.uniform(jax.random.fold_in(jax.random.fold_in(stream_key, 6), dim), (parts,), jnp.float32, smallest / len(cuts), top_value / len(cuts))
        gain = gain * jnp.repeat(jnp.exp(steps), dims[dim] // parts).reshape((-1,) + (1,) * (len(dims) - 1 - dim))
    return gain


def normal_values(stream_key, dims, deviation, limit, shards=(), kind=jnp.bfloat16):
    values = deviation * jax.random.normal(stream_key, dims, jnp.float32)
    if shards:
        values = values * block_scale(stream_key, dims, shards, -0.22, 0.18)
    return jnp.clip(values, -limit, limit).astype(kind)


def setup_inputs(seed: int = 0) -> dict:
    splits = jax.random.split(jax.random.key(seed), 5)
    return {
        "frames": normal_values(splits[0], (C, FRAMES, H * W), 1.0, 6.0, ((1, 4), (2, 8))),
        "weight": normal_values(splits[1], (C, 3, 3, C), (9 * C) ** -0.5, 0.09375, ((0, 2),)),
        "bias": normal_values(splits[2], (C,), 0.5, 3.0, (), jnp.float32),
        "cotangent": normal_values(splits[3], (C, FRAMES, H * W), 1.0, 6.0, ((1, 4), (2, 8))),
    }


def reference(frames, weight, bias, cotangent):
    channels, frame_count, cell_total = frames.shape
    row_count = cell_total // W
    inputs = frames.astype(jnp.float32).reshape(channels, frame_count, row_count, W)
    kernel = weight.astype(jnp.float32)
    upstream = cotangent.astype(jnp.float32).reshape(channels, frame_count, row_count, W)
    margin = ((0, 0), (0, 0), (1, 1), (1, 1))
    padded_in = jnp.pad(inputs, margin)
    padded_cot = jnp.pad(upstream, margin)
    scale = 1.0 / math.sqrt(frame_count * row_count * W)
    running = jnp.zeros(inputs.shape, jnp.float32) + bias[:, None, None, None]
    grad_in = jnp.zeros(inputs.shape, jnp.float32)
    tap_rows = []
    for a in range(3):
        tap_row = []
        for b in range(3):
            window = padded_in[:, :, a:a + row_count, b:b + W]
            running = running + jnp.einsum('ifhw,oi->ofhw', window, kernel[:, a, b, :])
            back = padded_cot[:, :, 2 - a:2 - a + row_count, 2 - b:2 - b + W]
            grad_in = grad_in + jnp.einsum('ofhw,oi->ifhw', back, kernel[:, a, b, :])
            tap_row.append(jnp.einsum('ifhw,ofhw->oi', window, upstream))
        tap_rows.append(jnp.stack(tap_row, axis=1))
    grad_weight = jnp.stack(tap_rows, axis=1) * scale
    grad_bias = lax.optimization_barrier(jnp.sum(upstream, axis=(1, 2, 3))) * scale
    outputs = running.reshape(channels, frame_count, cell_total).astype(jnp.bfloat16)
    grad_frames = grad_in.reshape(channels, frame_count, cell_total).astype(jnp.bfloat16)
    return (outputs, grad_frames, grad_weight, grad_bias)
```

```python
import functools
import math

import jax
import jax.numpy as jnp
from jax import lax
from jax.experimental import pallas as pl
from jax.experimental.pallas import tpu as pltpu
from jax.sharding import PartitionSpec as P

W = 160
MESH = pl.DeviceIdType.MESH


def ds(start, size):
    return pl.ds(pl.multiple_of(start, size), size)


def remote(src, dst, send, recv, device):
    return pltpu.make_async_remote_copy(
        src_ref=src, dst_ref=dst, send_sem=send, recv_sem=recv, device_id=device, device_id_type=MESH
    )


def position():
    return lax.axis_index("clip"), lax.axis_index("band"), lax.axis_index("chan")


def gather_kernel(dims, x_ref, g_ref, xs_ref, gs_ref, xsend, xrecv, gsend, grecv, fsend, frecv, own):
    bands, chans, rows_i, rows_o, cells = dims
    group = bands * chans
    _, b, n = position()
    me = b * chans + n
    sib = b + 1 - 2 * (b % 2)
    barrier = pltpu.get_barrier_semaphore()
    for k in range(1, group):
        to = (me + k) % group
        pl.semaphore_signal(barrier, inc=1, device_id={"band": to // chans, "chan": to % chans}, device_id_type=MESH)
    pl.semaphore_wait(barrier, group - 1)

    keep_x = pltpu.make_async_copy(x_ref.at[ds(b * rows_i, rows_i), :], xs_ref.at[:, ds(me * cells, cells)], own.at[0])
    keep_g = pltpu.make_async_copy(g_ref.at[ds(n * rows_o, rows_o), :], gs_ref.at[:, ds(me * cells, cells)], own.at[1])
    keep_x.start()
    keep_g.start()
    pairs = [(j, m) for j in range(bands // 2) for m in range(chans)]
    started = []
    for t, (j, m) in enumerate(pairs):
        if t == 0:
            continue
        to_b, to_n = (b + 2 * j) % bands, (n + m) % chans
        copy = remote(
            g_ref.at[ds(to_n * rows_o, rows_o), :], gs_ref.at[:, ds(me * cells, cells)],
            gsend.at[t], grecv.at[t], {"band": to_b, "chan": to_n},
        )
        copy.start()
        started.append(copy)
    for k in range(1, group):
        to = (me + k) % group
        to_b, to_n = to // chans, to % chans
        copy = remote(
            x_ref.at[ds(to_b * rows_i, rows_i), :], xs_ref.at[:, ds(me * cells, cells)],
            xsend.at[k], xrecv.at[k], {"band": to_b, "chan": to_n},
        )
        copy.start()
        started.append(copy)
    for t, (j, m) in enumerate(pairs):
        src = ((b + bands - 2 * j) % bands) * chans + (n + chans - m) % chans
        place = gs_ref.at[:, ds(src * cells, cells)]
        if t == 0:
            out = g_ref.at[ds(n * rows_o, rows_o), :]
        else:
            remote(place, place, gsend.at[t], grecv.at[t], {"band": sib}).wait_recv()
            out = place
        copy = remote(out, place, fsend.at[t], frecv.at[t], {"band": sib})
        copy.start()
        started.append(copy)
    for k in range(1, group):
        src = (me + group - k) % group
        place = xs_ref.at[:, ds(src * cells, cells)]
        remote(place, place, xsend.at[k], xrecv.at[k], {"band": sib}).wait_recv()
    for t, (j, m) in enumerate(pairs):
        src = ((sib + bands - 2 * j) % bands) * chans + (n + chans - m) % chans
        place = gs_ref.at[:, ds(src * cells, cells)]
        remote(place, place, fsend.at[t], frecv.at[t], {"band": sib}).wait_recv()
    for copy in started:
        copy.wait_send()
    keep_x.wait()
    keep_g.wait()


def share_kernel(
    dims, s_ref, d_ref, w_ref, lead_ref, last_ref, o_ref, db_ref, kern_ref, before_ref, after_ref,
    got, dgot, rsend, rrecv, dsend, drecv, wsend, wrecv, wfsend, wfrecv, hsend, hrecv,
    zsend, zrecv, xsend, xrecv, csend, crecv, own,
):
    clips, bands, chans, rows_o, rows_i = dims
    group = bands * chans
    taps = s_ref.shape[0]
    piece = rows_o // clips
    half = rows_o // 2
    z, b, n = position()
    me = b * chans + n
    core = b % 2
    sib = b + 1 - 2 * core
    nxt, prv = (me + 1) % group, (me + group - 1) % group
    nxt_id = {"band": nxt // chans, "chan": nxt % chans}
    prv_id = {"band": prv // chans, "chan": prv % chans}

    barrier = pltpu.get_barrier_semaphore()
    targets = [{"clip": (z + k) % clips} for k in range(1, clips)]
    targets += [{"chan": (n + m) % chans} for m in range(1, chans)]
    targets += [{"band": (b + 2 * j) % bands} for j in range(1, bands // 2)]
    targets += [{"band": sib}, nxt_id, prv_id]
    for target in targets:
        pl.semaphore_signal(barrier, inc=1, device_id=target, device_id_type=MESH)
    pl.semaphore_wait(barrier, len(targets))

    started = []

    def send(*args):
        copy = remote(*args)
        copy.start()
        started.append(copy)

    for k in range(1, clips):
        to = (z + k) % clips
        send(s_ref.at[:, ds(to * piece, piece), :], got.at[k], rsend.at[k], rrecv.at[k], {"clip": to})
        send(d_ref, dgot.at[k], dsend.at[k], drecv.at[k], {"clip": to})
    for m in range(1, chans):
        send(
            w_ref.at[:, ds(core * half, half), :], kern_ref.at[:, ds((2 * n + core) * half, half), :],
            wsend.at[m], wrecv.at[m], {"chan": (n + m) % chans},
        )
    send(last_ref, before_ref, hsend.at[0], hrecv.at[0], nxt_id)
    send(lead_ref, after_ref, hsend.at[1], hrecv.at[1], prv_id)
    keep_w = pltpu.make_async_copy(w_ref, kern_ref.at[:, ds(n * rows_o, rows_o), :], own)
    keep_w.start()

    for k in range(1, clips):
        remote(got.at[k], got.at[k], rsend.at[k], rrecv.at[k], {"band": sib}).wait_recv()
        remote(d_ref, dgot.at[k], dsend.at[k], drecv.at[k], {"band": sib}).wait_recv()

    def spot(zz, bb):
        return o_ref.at[:, ds(zz * piece, piece), ds(bb * rows_i, rows_i)]

    @pl.loop(0, taps)
    def _(t):
        total = s_ref[t, ds(z * piece, piece), :]
        for k in range(1, clips):
            total = total + got[k, t]
        o_ref[t, ds(z * piece, piece), ds(b * rows_i, rows_i)] = total

    db_total = d_ref[...]
    for k in range(1, clips):
        db_total = db_total + dgot[k]
    db_ref[...] = db_total

    width = bands // 2
    for k in range(clips):
        zz = (z + clips - k) % clips
        if k == 0:
            for q in range(1, clips):
                send(spot(z, b), spot(z, b), zsend.at[q], zrecv.at[q], {"clip": (z + q) % clips})
        else:
            remote(spot(zz, b), spot(zz, b), zsend.at[k], zrecv.at[k], {"band": sib}).wait_recv()
        for j in range(1, width):
            send(spot(zz, b), spot(zz, b), xsend.at[j, k], xrecv.at[j, k], {"band": (b + 2 * j) % bands})
        send(spot(zz, b), spot(zz, b), csend.at[0, k], crecv.at[0, k], {"band": sib})
    for m in range(1, chans):
        src = (n + chans - m) % chans
        place = kern_ref.at[:, ds((2 * src + core) * half, half), :]
        remote(place, place, wsend.at[m], wrecv.at[m], {"band": sib}).wait_recv()
        send(place, place, wfsend.at[m], wfrecv.at[m], {"band": sib})
    for k in range(clips):
        zz = (z + clips - k) % clips
        for j in range(1, width):
            bb = (b + bands - 2 * j) % bands
            remote(spot(zz, bb), spot(zz, bb), xsend.at[j, k], xrecv.at[j, k], {"band": sib}).wait_recv()
            send(spot(zz, bb), spot(zz, bb), csend.at[j, k], crecv.at[j, k], {"band": sib})
    for k in range(clips):
        zz = (z + clips - k) % clips
        for j in range(width):
            bb = (sib + bands - 2 * j) % bands
            remote(spot(zz, bb), spot(zz, bb), csend.at[j, k], crecv.at[j, k], {"band": sib}).wait_recv()
    for m in range(1, chans):
        src = (n + chans - m) % chans
        place = kern_ref.at[:, ds((2 * src + 1 - core) * half, half), :]
        remote(place, place, wfsend.at[m], wfrecv.at[m], {"band": sib}).wait_recv()
    remote(last_ref, before_ref, hsend.at[0], hrecv.at[0], {"band": sib}).wait_recv()
    remote(lead_ref, after_ref, hsend.at[1], hrecv.at[1], {"band": sib}).wait_recv()
    for copy in started:
        copy.wait_send()
    keep_w.wait()


VM = pl.BlockSpec(memory_space=pltpu.VMEM)
DMA = pltpu.SemaphoreType.DMA


def local(frames, weight, bias, cotangent):
    channels, frame_count, cells = frames.shape
    clips, bands, chans = (lax.axis_size(a) for a in ("clip", "band", "chan"))
    group = bands * chans
    assert frame_count == 1 and cells % W == 0
    total = cells * group
    scale = 1.0 / math.sqrt(frame_count * clips * total)
    rows_i, rows_o = channels // bands, channels // chans
    x = frames.reshape(channels, cells)
    g = cotangent.reshape(channels, cells)
    bf = jnp.bfloat16
    pairs = bands // 2 * chans
    xs, gs = pl.pallas_call(
        functools.partial(gather_kernel, (bands, chans, rows_i, rows_o, cells)),
        out_shape=(jax.ShapeDtypeStruct((rows_i, total), bf), jax.ShapeDtypeStruct((rows_o, total), bf)),
        in_specs=[VM, VM],
        out_specs=(VM, VM),
        scratch_shapes=[DMA((group,)), DMA((group,)), DMA((pairs,)), DMA((pairs,)), DMA((pairs,)), DMA((pairs,)), DMA((2,))],
        compiler_params=pltpu.CompilerParams(collective_id=0, has_side_effects=True),
    )(x, g)

    column = jnp.arange(total, dtype=jnp.int32) % W
    margin = jnp.zeros((rows_i, W), bf)
    zero = jnp.zeros((), bf)
    sides = []
    for b in range(3):
        moved = xs if b == 1 else jnp.roll(xs, 1 - b, axis=1)
        if b != 1:
            moved = jnp.where((column != (0 if b == 0 else W - 1))[None, :], moved, zero)
        sides.append(jnp.concatenate([margin, moved, margin], axis=1))
    sides = jnp.concatenate(sides, axis=0)
    share = []
    for a in range(3):
        window = lax.slice_in_dim(sides, a * W, a * W + total, axis=1)
        part = lax.dot_general(gs, window, (((1,), (1,)), ((), ())), preferred_element_type=jnp.float32)
        share += [part[:, b * rows_i:(b + 1) * rows_i] * scale for b in range(3)]
    share = jnp.stack(share, axis=0)
    db = jnp.sum(gs.astype(jnp.float32), axis=1) * scale
    db = jnp.broadcast_to(db[None, :], (8, rows_o))

    lead = jnp.concatenate([x[:, :W], g[:, :W]], axis=1)
    last = jnp.concatenate([x[:, cells - W:], g[:, cells - W:]], axis=1)
    wt = jnp.transpose(weight, (1, 2, 0, 3)).reshape(9, rows_o, channels)
    piece = rows_o // clips
    width = bands // 2
    grad, db, kern, before, after = pl.pallas_call(
        functools.partial(share_kernel, (clips, bands, chans, rows_o, rows_i)),
        out_shape=(
            jax.ShapeDtypeStruct((9, rows_o, channels), jnp.float32),
            jax.ShapeDtypeStruct((8, rows_o), jnp.float32),
            jax.ShapeDtypeStruct((9, channels, channels), bf),
            jax.ShapeDtypeStruct((channels, 2 * W), bf),
            jax.ShapeDtypeStruct((channels, 2 * W), bf),
        ),
        in_specs=[VM] * 5,
        out_specs=(VM,) * 5,
        scratch_shapes=[
            pltpu.VMEM((clips, 9, piece, rows_i), jnp.float32),
            pltpu.VMEM((clips, 8, rows_o), jnp.float32),
        ] + [DMA((clips,))] * 4 + [DMA((chans,))] * 4 + [DMA((2,))] * 2 + [DMA((clips,))] * 2
        + [DMA((width, clips))] * 4 + [DMA],
        compiler_params=pltpu.CompilerParams(collective_id=1, has_side_effects=True, vmem_limit_bytes=48 << 20),
    )(share, db, wt, lead, last)

    index = lax.axis_index(("band", "chan"))
    before = jnp.where(index == 0, zero, before)
    after = jnp.where(index == group - 1, zero, after)
    pad = jnp.zeros((channels, 1), bf)
    ext_x = jnp.concatenate([pad, before[:, :W], x, after[:, :W], pad], axis=1)
    ext_g = jnp.concatenate([pad, before[:, W:], g, after[:, W:], pad], axis=1)
    column = jnp.arange(cells, dtype=jnp.int32) % W
    keep = (column != 0, None, column != W - 1)

    def window(source, a, b):
        start = 1 + a * W + b - 1
        part = lax.slice_in_dim(source, start, start + cells, axis=1)
        return part if keep[b] is None else jnp.where(keep[b][None, :], part, zero)

    conv = jnp.zeros((channels, cells), jnp.float32)
    back = jnp.zeros((channels, cells), jnp.float32)
    for a in range(3):
        for b in range(3):
            tap = kern[3 * a + b]
            conv = conv + lax.dot_general(tap, window(ext_x, a, b), (((1,), (0,)), ((), ())), preferred_element_type=jnp.float32)
            back = back + lax.dot_general(tap, window(ext_g, 2 - a, 2 - b), (((0,), (0,)), ((), ())), preferred_element_type=jnp.float32)
    outputs = (conv + bias[:, None]).astype(bf).reshape(frames.shape)
    grad_frames = back.astype(bf).reshape(frames.shape)
    grad_weight = jnp.transpose(grad.reshape(3, 3, rows_o, channels), (2, 0, 1, 3))
    return outputs, grad_frames, grad_weight, db[0]


def solution(mesh):
    cells = P(None, "clip", ("band", "chan"))
    kernel = P("chan", None, None, None)
    return jax.shard_map(
        local, mesh=mesh, in_specs=(cells, kernel, P(), cells), out_specs=(cells, cells, kernel, P("chan")), check_vma=False
    )
```

```python
import functools
import math

import jax
import jax.numpy as jnp
from jax import lax
from jax.experimental import pallas as pl
from jax.experimental.pallas import tpu as pltpu
from jax.sharding import PartitionSpec as P

W = 160
MESH = pl.DeviceIdType.MESH
F32 = jnp.float32
BF16 = jnp.bfloat16


def ds(start, size):
    return pl.ds(pl.multiple_of(start, size), size)


def remote(src, dst, send, recv, device):
    return pltpu.make_async_remote_copy(
        src_ref=src, dst_ref=dst, send_sem=send, recv_sem=recv, device_id=device, device_id_type=MESH
    )


def sides(rows):
    wide = rows.astype(F32)
    at = lax.broadcasted_iota(jnp.int32, wide.shape, 0)
    left = jnp.where(at == 0, 0.0, pltpu.roll(wide, 1, 0)).astype(BF16)
    right = jnp.where(at == W - 1, 0.0, pltpu.roll(wide, W - 1, 0)).astype(BF16)
    return left, rows, right


def kernel(
    dims, xt_ref, gt_ref, g_ref, w_ref, bias_ref, o_ref, db_ref, out_ref, back_ref,
    xs, gs, dx, xe, ge, kern, acc, share, got1, got2, dbs, dgot, hx, hg, sems, regs,
):
    clips, bands, chans, rows_o, rows_i, cells, channels, scale = dims
    group = bands * chans
    half = rows_o // 2
    lanes = channels // clips
    width = bands // 2
    units = cells // W
    total = cells * group
    z, b, n = lax.axis_index("clip"), lax.axis_index("band"), lax.axis_index("chan")
    me = b * chans + n
    core = b % 2
    sib = b + 1 - 2 * core
    sib_id = {"band": sib}
    nxt, prv = (me + 1) % group, (me + group - 1) % group
    nxt_id = {"band": nxt // chans, "chan": nxt % chans}
    prv_id = {"band": prv // chans, "chan": prv % chans}
    z0, z1 = z % 2, z // 2
    near, far = {"clip": z + 1 - 2 * z0}, {"clip": (z + 2) % clips}

    barrier = pltpu.get_barrier_semaphore()
    targets = [{"clip": (z + k) % clips} for k in range(1, clips)]
    for k in range(1, group):
        to = (me + k) % group
        targets.append({"band": to // chans, "chan": to % chans})
    for target in targets:
        pl.semaphore_signal(barrier, inc=1, device_id=target, device_id_type=MESH)
    pl.semaphore_wait(barrier, len(targets))

    started = []
    names = {}

    def pair(key):
        if key not in names:
            names[key] = len(names)
        return sems.at[0, names[key]], sems.at[1, names[key]]

    def send(src, dst, key, device):
        s, r = pair(key)
        copy = remote(src, dst, s, r, device)
        copy.start()
        started.append(copy)

    def arrive(dst, key):
        s, r = pair(key)
        remote(dst, dst, s, r, sib_id).wait_recv()

    def slab(src_n, part, zz):
        return kern.at[:, ds((2 * src_n + part) * half, half), ds(zz * lanes, lanes)]

    for m in range(1, chans):
        send(w_ref.at[:, ds(core * half, half), ds(z * lanes, lanes)], slab(n, core, z), ("w", m), {"chan": (n + m) % chans})
    keep_w = pltpu.make_async_copy(w_ref, kern.at[:, ds(n * rows_o, rows_o), :], regs.at[0])
    keep_w.start()
    keep_x = pltpu.make_async_copy(xt_ref.at[:, ds(b * rows_i, rows_i)], xs.at[ds(me * cells, cells), :], regs.at[1])
    keep_g = pltpu.make_async_copy(g_ref.at[ds(n * rows_o, rows_o), :], gs.at[:, ds(me * cells, cells)], regs.at[2])
    keep_x.start()
    keep_g.start()

    pairs = [(j, m) for j in range(width) for m in range(chans)]
    for j, m in pairs[1:]:
        to_b, to_n = (b + 2 * j) % bands, (n + m) % chans
        send(
            g_ref.at[ds(to_n * rows_o, rows_o), :], gs.at[:, ds(me * cells, cells)], ("g", j, m),
            {"band": to_b, "chan": to_n},
        )
    for k in range(1, group):
        to = (me + k) % group
        to_b, to_n = to // chans, to % chans
        send(
            xt_ref.at[:, ds(to_b * rows_i, rows_i)], xs.at[ds(me * cells, cells), :], ("x", k),
            {"band": to_b, "chan": to_n},
        )
    send(g_ref.at[ds(n * rows_o, rows_o), :], gs.at[:, ds(me * cells, cells)], ("f", 0, 0), sib_id)
    send(xt_ref.at[pl.ds(cells - W, W), :], hx.at[0], ("hx", 0), nxt_id)
    send(gt_ref.at[pl.ds(cells - W, W), :], hg.at[0], ("hg", 0), nxt_id)
    send(xt_ref.at[pl.ds(0, W), :], hx.at[1], ("hx", 1), prv_id)
    send(gt_ref.at[pl.ds(0, W), :], hg.at[1], ("hg", 1), prv_id)

    for m in range(1, chans):
        src = (n + chans - m) % chans
        arrive(slab(src, core, z), ("w", m))
        for q in range(1, clips):
            send(slab(src, core, z), slab(src, core, z), ("wz", m, q), {"clip": (z + q) % clips})
        send(slab(src, core, z), slab(src, core, z), ("ws", m, 0), sib_id)

    def widen(dst, to, rows, size):
        for t, part in enumerate(sides(rows)):
            dst[ds(to, W), t * size:(t + 1) * size] = part

    @pl.loop(0, units)
    def _(u):
        widen(xe, (u + 1) * W, xt_ref[ds(u * W, W), :], channels)
        widen(ge, (u + 1) * W, gt_ref[ds(u * W, W), :], channels)

    for j, m in pairs[1:]:
        src = ((b + bands - 2 * j) % bands) * chans + (n + chans - m) % chans
        place = gs.at[:, ds(src * cells, cells)]
        arrive(place, ("g", j, m))
        send(place, place, ("f", j, m), sib_id)
    for k in range(1, group):
        src = (me + group - k) % group
        arrive(xs.at[ds(src * cells, cells), :], ("x", k))
    keep_x.wait()
    dx[pl.ds(0, W), :] = jnp.zeros((W, 3 * rows_i), BF16)
    dx[pl.ds(total + W, W), :] = jnp.zeros((W, 3 * rows_i), BF16)

    @pl.loop(0, total // W)
    def _(u):
        widen(dx, (u + 1) * W, xs[ds(u * W, W), :], rows_i)

    for j, m in pairs:
        src = ((sib + bands - 2 * j) % bands) * chans + (n + chans - m) % chans
        arrive(gs.at[:, ds(src * cells, cells)], ("f", j, m))
    keep_g.wait()

    block = 2 * cells

    def tap_row(a):
        acc2 = acc.at[pl.ds(0, rows_o), pl.ds(0, 3 * rows_i)]
        acc2[...] = jnp.zeros((rows_o, 3 * rows_i), F32)

        @pl.loop(0, group // 2)
        def _(k):
            rows = pl.ds(pl.multiple_of(k * block + a * W, 32), block)
            acc2[...] += jnp.dot(gs[:, ds(k * block, block)], dx[rows, :], preferred_element_type=F32)

        for t in range(3):
            share[3 * a + t] = acc2[:, t * rows_i:(t + 1) * rows_i] * scale
        taps = pl.ds(3 * a, 3)
        send(share.at[taps, ds((1 - z0) * half, half), :], got1.at[taps], ("r1", a), near)

    quarter = half // 2

    def spot(a, start, size, bb):
        return o_ref.at[pl.ds(3 * a, 3), ds(start, size), ds(bb * rows_i, rows_i)]

    def reduce1(a):
        arrive(got1.at[pl.ds(3 * a, 3)], ("r1", a))
        for t in range(3 * a, 3 * a + 3):
            share[t, ds(z0 * half, half), :] += got1[t]
        send(
            share.at[pl.ds(3 * a, 3), ds((2 * z0 + 1 - z1) * quarter, quarter), :],
            got2.at[pl.ds(3 * a, 3)], ("r2", a), far,
        )

    def spread(a, start, size, step):
        place = spot(a, start, size, b)
        for j in range(1, width):
            send(place, place, ("xo", a, step, j), {"band": (b + 2 * j) % bands})
        send(place, place, ("c", a, step, 0), sib_id)

    mine = (2 * z0 + z1) * quarter
    other = (2 * z0 + 1 - z1) * quarter

    def reduce2(a):
        arrive(got2.at[pl.ds(3 * a, 3)], ("r2", a))
        for t in range(3 * a, 3 * a + 3):
            o_ref[t, ds(mine, quarter), ds(b * rows_i, rows_i)] = share[t, ds(mine, quarter), :] + got2[t]
        send(spot(a, mine, quarter, b), spot(a, mine, quarter, b), ("a1", a), far)
        spread(a, mine, quarter, 0)

    def gather1(a):
        arrive(spot(a, other, quarter, b), ("a1", a))
        send(spot(a, z0 * half, half, b), spot(a, z0 * half, half, b), ("a2", a), near)
        spread(a, other, quarter, 1)

    def gather2(a):
        arrive(spot(a, (1 - z0) * half, half, b), ("a2", a))
        spread(a, (1 - z0) * half, half, 2)

    def regions(step):
        return ((mine, quarter), (other, quarter), ((1 - z0) * half, half))[step]

    def cross(a):
        for step in range(3):
            start, size = regions(step)
            for j in range(1, width):
                place = spot(a, start, size, (b + bands - 2 * j) % bands)
                arrive(place, ("xo", a, step, j))
                send(place, place, ("c", a, step, j), sib_id)

    def finish(a):
        for step in range(3):
            start, size = regions(step)
            for j in range(width):
                arrive(spot(a, start, size, (sib + bands - 2 * j) % bands), ("c", a, step, j))

    def conv(a):
        @pl.loop(0, channels // 256)
        def _(t):
            rows = ds(t * 256, 256)
            part = jnp.zeros((256, cells), F32) + bias_ref[rows, :] if a == 0 else acc[rows, :]
            for s in range(3):
                part += lax.dot_general(
                    kern[3 * a + s, rows, :], xe[a * W:a * W + cells, s * channels:(s + 1) * channels],
                    (((1,), (1,)), ((), ())), preferred_element_type=F32,
                )
            if a == 2:
                out_ref[rows, :] = part.astype(BF16)
            else:
                acc[rows, :] = part

    half_cells = cells // 2

    def back(a):
        @pl.loop(0, 2)
        def _(t):
            rows = ds(t * half_cells, half_cells)
            c = 2 - a
            part = jnp.zeros((half_cells, channels), F32)
            if a:
                part = acc[ds(t * half_cells, half_cells), pl.ds(0, channels)]
            for s in range(3):
                part += jnp.dot(
                    ge[pl.ds(pl.multiple_of(c * W + t * half_cells, 32), half_cells), (2 - s) * channels:(3 - s) * channels],
                    kern[3 * a + s], preferred_element_type=F32,
                )
            if a == 2:
                back_ref[rows, :] = part.astype(BF16)
            else:
                acc[rows, pl.ds(0, channels)] = part

    def bias_sum():
        ones = jnp.ones((8, block), BF16)
        dbs[...] = jnp.zeros((8, rows_o), F32)

        @pl.loop(0, group // 2)
        def _(k):
            dbs[...] += lax.dot_general(
                ones, gs[:, ds(k * block, block)], (((1,), (1,)), ((), ())), preferred_element_type=F32
            )

        for q in range(1, clips):
            send(dbs, dgot.at[q], ("d", q), {"clip": (z + q) % clips})

    def halos():
        for h in range(2):
            arrive(hx.at[h], ("hx", h))
            arrive(hg.at[h], ("hg", h))
            edge = me == (0 if h == 0 else group - 1)
            for src, dst in ((hx, xe), (hg, ge)):
                rows = src[h]
                rows = jnp.where(edge, jnp.zeros_like(rows), rows)
                for t, part in enumerate(sides(rows)):
                    dst[pl.ds(h * (cells + W), W), t * channels:(t + 1) * channels] = part

    def weights():
        for m in range(1, chans):
            src = (n + chans - m) % chans
            for q in range(1, clips):
                zz = (z + clips - q) % clips
                arrive(slab(src, core, zz), ("wz", m, q))
                send(slab(src, core, zz), slab(src, core, zz), ("ws", m, q), sib_id)
        for m in range(1, chans):
            src = (n + chans - m) % chans
            for q in range(clips):
                arrive(slab(src, 1 - core, (z + clips - q) % clips), ("ws", m, q))
        keep_w.wait()

    tap_row(0)
    tap_row(1)
    reduce1(0)
    tap_row(2)
    bias_sum()
    reduce1(1)
    halos()
    reduce2(0)
    reduce1(2)
    weights()
    conv(0)
    reduce2(1)
    gather1(0)
    conv(1)
    reduce2(2)
    gather1(1)
    conv(2)
    gather2(0)
    gather1(2)
    back(0)
    gather2(1)
    cross(0)
    back(1)
    gather2(2)
    cross(1)
    back(2)
    cross(2)
    for q in range(1, clips):
        arrive(dgot.at[q], ("d", q))
    sums = dbs[...]
    for q in range(1, clips):
        sums = sums + dgot[q]
    db_ref[...] = sums * scale
    for a in range(3):
        finish(a)
    for copy in started:
        copy.wait_send()


VM = pl.BlockSpec(memory_space=pltpu.VMEM)


def local(frames, weight, bias, cotangent):
    channels, frame_count, cells = frames.shape
    clips, bands, chans = (lax.axis_size(a) for a in ("clip", "band", "chan"))
    group = bands * chans
    assert frame_count == 1 and cells % W == 0 and clips == 4
    total = cells * group
    scale = 1.0 / math.sqrt(frame_count * clips * total)
    rows_i, rows_o = channels // bands, channels // chans
    x = frames.reshape(channels, cells)
    g = cotangent.reshape(channels, cells)
    wt = jnp.transpose(weight, (1, 2, 0, 3)).reshape(9, rows_o, channels)
    half = rows_o // 2
    width = bands // 2
    copies = (chans - 1) * (1 + clips - 1 + clips) + 2 * width * chans + group + 4 + 12 + clips + 9 * (2 * width) + 8
    shape = jax.ShapeDtypeStruct
    grad, db, outputs, back = pl.pallas_call(
        functools.partial(kernel, (clips, bands, chans, rows_o, rows_i, cells, channels, scale)),
        out_shape=(
            shape((9, rows_o, channels), F32),
            shape((8, rows_o), F32),
            shape((channels, cells), BF16),
            shape((cells, channels), BF16),
        ),
        in_specs=[VM] * 5,
        out_specs=(VM,) * 4,
        scratch_shapes=[
            pltpu.VMEM((total, rows_i), BF16),
            pltpu.VMEM((rows_o, total), BF16),
            pltpu.VMEM((total + 2 * W, 3 * rows_i), BF16),
            pltpu.VMEM((cells + 2 * W, 3 * channels), BF16),
            pltpu.VMEM((cells + 2 * W, 3 * channels), BF16),
            pltpu.VMEM((9, channels, channels), BF16),
            pltpu.VMEM((max(channels, cells), max(channels, cells)), F32),
            pltpu.VMEM((9, rows_o, rows_i), F32),
            pltpu.VMEM((9, half, rows_i), F32),
            pltpu.VMEM((9, half // 2, rows_i), F32),
            pltpu.VMEM((8, rows_o), F32),
            pltpu.VMEM((clips, 8, rows_o), F32),
            pltpu.VMEM((2, W, channels), BF16),
            pltpu.VMEM((2, W, channels), BF16),
            pltpu.SemaphoreType.DMA((2, copies)),
            pltpu.SemaphoreType.DMA((3,)),
        ],
        compiler_params=pltpu.CompilerParams(collective_id=0, has_side_effects=True, vmem_limit_bytes=67000000),
    )(x.T, g.T, g, wt, bias[:, None])
    outputs = outputs.reshape(frames.shape)
    grad_frames = back.T.reshape(frames.shape)
    grad_weight = jnp.transpose(grad.reshape(3, 3, rows_o, channels), (2, 0, 1, 3))
    return outputs, grad_frames, grad_weight, db[0]


def solution(mesh):
    cells = P(None, "clip", ("band", "chan"))
    taps = P("chan", None, None, None)
    return jax.shard_map(
        local, mesh=mesh, in_specs=(cells, taps, P(), cells), out_specs=(cells, cells, taps, P("chan")), check_vma=False
    )
```

```python
import functools
import math

import jax
import jax.numpy as jnp
from jax import lax
from jax.experimental import pallas as pl
from jax.experimental.pallas import tpu as pltpu
from jax.sharding import PartitionSpec as P

W = 160
MESH = pl.DeviceIdType.MESH
F32 = jnp.float32
BF16 = jnp.bfloat16


def ds(start, size):
    return pl.ds(pl.multiple_of(start, size), size)


def remote(src, dst, send, recv, device):
    return pltpu.make_async_remote_copy(
        src_ref=src, dst_ref=dst, send_sem=send, recv_sem=recv, device_id=device, device_id_type=MESH
    )


def sides(rows):
    wide = rows.astype(F32)
    at = lax.broadcasted_iota(jnp.int32, wide.shape, 0)
    left = jnp.where(at == 0, 0.0, pltpu.roll(wide, 1, 0)).astype(BF16)
    right = jnp.where(at == W - 1, 0.0, pltpu.roll(wide, W - 1, 0)).astype(BF16)
    return left, rows, right


def kernel(
    dims, x_ref, g_ref, w_ref, bias_ref, o_ref, db_ref, out_ref, back_ref,
    xs, gs, dx, xe, ge, kern, acc, share, got1, got2, dbs, dgot, hx, hg, xt_ref, gt_ref, sems, regs,
):
    clips, bands, chans, rows_o, rows_i, cells, channels, scale = dims
    group = bands * chans
    half = rows_o // 2
    lanes = channels // clips
    width = bands // 2
    units = cells // W
    total = cells * group
    z, b, n = lax.axis_index("clip"), lax.axis_index("band"), lax.axis_index("chan")
    me = b * chans + n
    core = b % 2
    sib = b + 1 - 2 * core
    sib_id = {"band": sib}
    nxt, prv = (me + 1) % group, (me + group - 1) % group
    nxt_id = {"band": nxt // chans, "chan": nxt % chans}
    prv_id = {"band": prv // chans, "chan": prv % chans}
    z0, z1 = z % 2, z // 2
    near, far = {"clip": z + 1 - 2 * z0}, {"clip": (z + 2) % clips}

    barrier = pltpu.get_barrier_semaphore()
    targets = [{"clip": (z + k) % clips} for k in range(1, clips)]
    for k in range(1, group):
        to = (me + k) % group
        targets.append({"band": to // chans, "chan": to % chans})
    for target in targets:
        pl.semaphore_signal(barrier, inc=1, device_id=target, device_id_type=MESH)

    def turn(src, dst):
        @pl.loop(0, cells // 128)
        def _(t):
            dst[ds(t * 128, 128), :] = src[:, ds(t * 128, 128)].astype(F32).T.astype(BF16)

    turn(x_ref, xt_ref)
    pl.semaphore_wait(barrier, len(targets))

    started = []
    names = {}

    def pair(key):
        if key not in names:
            names[key] = len(names)
        return sems.at[0, names[key]], sems.at[1, names[key]]

    def send(src, dst, key, device):
        s, r = pair(key)
        copy = remote(src, dst, s, r, device)
        copy.start()
        started.append(copy)

    def arrive(dst, key):
        s, r = pair(key)
        remote(dst, dst, s, r, sib_id).wait_recv()

    def slab(src_n, part, zz):
        return kern.at[:, ds((2 * src_n + part) * half, half), ds(zz * lanes, lanes)]

    keep_w = pltpu.make_async_copy(w_ref, kern.at[:, ds(n * rows_o, rows_o), :], regs.at[0])
    keep_x = pltpu.make_async_copy(xt_ref.at[:, ds(b * rows_i, rows_i)], xs.at[ds(me * cells, cells), :], regs.at[1])
    keep_g = pltpu.make_async_copy(g_ref.at[ds(n * rows_o, rows_o), :], gs.at[:, ds(me * cells, cells)], regs.at[2])

    def x_place(src_b, src_n):
        return xs.at[ds((src_b * chans + src_n) * cells, cells), :]

    def g_place(src_b, src_n):
        return gs.at[:, ds((src_b * chans + src_n) * cells, cells)]

    for d in range(1, bands):
        to_b = (b + d) % bands
        send(xt_ref.at[:, ds(to_b * rows_i, rows_i)], x_place(b, n), ("x", d, 0), {"band": to_b})
    for m in range(1, chans):
        to_n = (n + m) % chans
        send(g_ref.at[ds(to_n * rows_o, rows_o), :], g_place(b, n), ("g", 0, m), {"chan": to_n})
        send(xt_ref.at[:, ds(b * rows_i, rows_i)], x_place(b, n), ("x", 0, m), {"chan": to_n})
    for m in range(1, chans):
        send(w_ref.at[:, ds(core * half, half), ds(z * lanes, lanes)], slab(n, core, z), ("w", m), {"chan": (n + m) % chans})
    own_g = g_ref.at[ds(n * rows_o, rows_o), :]
    for j in range(1, width):
        send(own_g, g_place(b, n), ("g", j, 0), {"band": (b + 2 * j) % bands})
    send(own_g, g_place(b, n), ("f", 0, 0), sib_id)
    keep_x.start()
    keep_g.start()
    keep_w.start()

    def widen(dst, to, rows, size):
        for t, part in enumerate(sides(rows)):
            dst[ds(to, W), t * size:(t + 1) * size] = part

    def widen_block(src):
        @pl.loop(0, units)
        def _(u):
            at = src * cells + u * W
            widen(dx, at + W, xs[ds(at, W), :], rows_i)

    for d in range(1, bands):
        place = x_place((b + bands - d) % bands, n)
        arrive(place, ("x", d, 0))
        for m in range(1, chans):
            send(place, place, ("x", d, m), {"chan": (n + m) % chans})
    for m in range(1, chans):
        place = g_place(b, (n + chans - m) % chans)
        arrive(place, ("g", 0, m))
        for j in range(1, width):
            send(place, place, ("g", j, m), {"band": (b + 2 * j) % bands})
        send(place, place, ("f", 0, m), sib_id)
    for m in range(1, chans):
        src = (n + chans - m) % chans
        arrive(slab(src, core, z), ("w", m))
        for q in range(1, clips):
            send(slab(src, core, z), slab(src, core, z), ("wz", m, q), {"clip": (z + q) % clips})
        send(slab(src, core, z), slab(src, core, z), ("ws", m, 0), sib_id)
    for j in range(1, width):
        place = g_place((b + bands - 2 * j) % bands, n)
        arrive(place, ("g", j, 0))
        send(place, place, ("f", j, 0), sib_id)

    turn(g_ref, gt_ref)
    dx[pl.ds(0, W), :] = jnp.zeros((W, 3 * rows_i), BF16)
    dx[pl.ds(total + W, W), :] = jnp.zeros((W, 3 * rows_i), BF16)

    @pl.loop(0, units)
    def _(u):
        widen(xe, (u + 1) * W, xt_ref[ds(u * W, W), :], channels)
        widen(ge, (u + 1) * W, gt_ref[ds(u * W, W), :], channels)

    keep_x.wait()
    widen_block(me)
    for d in range(1, bands):
        widen_block(((b + bands - d) % bands) * chans + n)
    for m in range(1, chans):
        src_n = (n + chans - m) % chans
        arrive(x_place(b, src_n), ("x", 0, m))
        widen_block(b * chans + src_n)
    for j in range(1, width):
        for m in range(1, chans):
            place = g_place((b + bands - 2 * j) % bands, (n + chans - m) % chans)
            arrive(place, ("g", j, m))
            send(place, place, ("f", j, m), sib_id)
    for d in range(1, bands):
        for m in range(1, chans):
            src_b, src_n = (b + bands - d) % bands, (n + chans - m) % chans
            arrive(x_place(src_b, src_n), ("x", d, m))
            widen_block(src_b * chans + src_n)
    send(xt_ref.at[pl.ds(cells - W, W), :], hx.at[0], ("hx", 0), nxt_id)
    send(gt_ref.at[pl.ds(cells - W, W), :], hg.at[0], ("hg", 0), nxt_id)
    send(xt_ref.at[pl.ds(0, W), :], hx.at[1], ("hx", 1), prv_id)
    send(gt_ref.at[pl.ds(0, W), :], hg.at[1], ("hg", 1), prv_id)
    for j in range(width):
        for m in range(chans):
            arrive(g_place((sib + bands - 2 * j) % bands, (n + chans - m) % chans), ("f", j, m))
    keep_g.wait()

    block = 2 * cells

    def tap_row(a):
        acc2 = acc.at[pl.ds(0, rows_o), pl.ds(0, 3 * rows_i)]
        acc2[...] = jnp.zeros((rows_o, 3 * rows_i), F32)

        @pl.loop(0, group // 2)
        def _(k):
            rows = pl.ds(pl.multiple_of(k * block + a * W, 32), block)
            acc2[...] += jnp.dot(gs[:, ds(k * block, block)], dx[rows, :], preferred_element_type=F32)

        for t in range(3):
            share[3 * a + t] = acc2[:, t * rows_i:(t + 1) * rows_i] * scale
        taps = pl.ds(3 * a, 3)
        send(share.at[taps, ds((1 - z0) * half, half), :], got1.at[taps], ("r1", a), near)

    quarter = half // 2

    def spot(a, start, size, bb):
        return o_ref.at[pl.ds(3 * a, 3), ds(start, size), ds(bb * rows_i, rows_i)]

    def reduce1(a):
        arrive(got1.at[pl.ds(3 * a, 3)], ("r1", a))
        for t in range(3 * a, 3 * a + 3):
            share[t, ds(z0 * half, half), :] += got1[t]
        send(
            share.at[pl.ds(3 * a, 3), ds((2 * z0 + 1 - z1) * quarter, quarter), :],
            got2.at[pl.ds(3 * a, 3)], ("r2", a), far,
        )

    def spread(a, start, size, step):
        place = spot(a, start, size, b)
        for j in range(1, width):
            send(place, place, ("xo", a, step, j), {"band": (b + 2 * j) % bands})
        send(place, place, ("c", a, step, 0), sib_id)

    mine = (2 * z0 + z1) * quarter
    other = (2 * z0 + 1 - z1) * quarter

    def reduce2(a):
        arrive(got2.at[pl.ds(3 * a, 3)], ("r2", a))
        for t in range(3 * a, 3 * a + 3):
            o_ref[t, ds(mine, quarter), ds(b * rows_i, rows_i)] = share[t, ds(mine, quarter), :] + got2[t]
        send(spot(a, mine, quarter, b), spot(a, mine, quarter, b), ("a1", a), far)
        spread(a, mine, quarter, 0)

    def gather1(a):
        arrive(spot(a, other, quarter, b), ("a1", a))
        send(spot(a, z0 * half, half, b), spot(a, z0 * half, half, b), ("a2", a), near)
        spread(a, other, quarter, 1)

    def gather2(a):
        arrive(spot(a, (1 - z0) * half, half, b), ("a2", a))
        spread(a, (1 - z0) * half, half, 2)

    def regions(step):
        return ((mine, quarter), (other, quarter), ((1 - z0) * half, half))[step]

    def cross(a):
        for step in range(3):
            start, size = regions(step)
            for j in range(1, width):
                place = spot(a, start, size, (b + bands - 2 * j) % bands)
                arrive(place, ("xo", a, step, j))
                send(place, place, ("c", a, step, j), sib_id)

    def finish(a):
        for step in range(3):
            start, size = regions(step)
            for j in range(width):
                arrive(spot(a, start, size, (sib + bands - 2 * j) % bands), ("c", a, step, j))

    def conv(a):
        @pl.loop(0, channels // 256)
        def _(t):
            rows = ds(t * 256, 256)
            if a == 0:
                column = jnp.broadcast_to(bias_ref[:, rows], (8, 256)).T[:, :1]
                part = jnp.zeros((256, cells), F32) + column
            else:
                part = acc[rows, :]
            for s in range(3):
                part += lax.dot_general(
                    kern[3 * a + s, rows, :], xe[a * W:a * W + cells, s * channels:(s + 1) * channels],
                    (((1,), (1,)), ((), ())), preferred_element_type=F32,
                )
            if a == 2:
                out_ref[rows, :] = part.astype(BF16)
            else:
                acc[rows, :] = part

    half_cells = cells // 2

    def back(a):
        @pl.loop(0, 2)
        def _(t):
            rows = ds(t * half_cells, half_cells)
            c = 2 - a
            part = jnp.zeros((half_cells, channels), F32)
            if a:
                part = acc[ds(t * half_cells, half_cells), pl.ds(0, channels)]
            for s in range(3):
                part += jnp.dot(
                    ge[pl.ds(pl.multiple_of(c * W + t * half_cells, 32), half_cells), (2 - s) * channels:(3 - s) * channels],
                    kern[3 * a + s], preferred_element_type=F32,
                )
            acc[rows, pl.ds(0, channels)] = part

        if a == 2:
            @pl.loop(0, cells // 128)
            def _(t):
                back_ref[:, ds(t * 128, 128)] = acc[ds(t * 128, 128), pl.ds(0, channels)].T.astype(BF16)

    def bias_sum():
        ones = jnp.ones((8, block), BF16)
        dbs[...] = jnp.zeros((8, rows_o), F32)

        @pl.loop(0, group // 2)
        def _(k):
            dbs[...] += lax.dot_general(
                ones, gs[:, ds(k * block, block)], (((1,), (1,)), ((), ())), preferred_element_type=F32
            )

        for q in range(1, clips):
            send(dbs, dgot.at[q], ("d", q), {"clip": (z + q) % clips})

    def halos():
        for h in range(2):
            arrive(hx.at[h], ("hx", h))
            arrive(hg.at[h], ("hg", h))
            edge = me == (0 if h == 0 else group - 1)
            for src, dst in ((hx, xe), (hg, ge)):
                rows = src[h]
                rows = jnp.where(edge, jnp.zeros_like(rows), rows)
                for t, part in enumerate(sides(rows)):
                    dst[pl.ds(h * (cells + W), W), t * channels:(t + 1) * channels] = part

    def weights():
        for m in range(1, chans):
            src = (n + chans - m) % chans
            for q in range(1, clips):
                zz = (z + clips - q) % clips
                arrive(slab(src, core, zz), ("wz", m, q))
                send(slab(src, core, zz), slab(src, core, zz), ("ws", m, q), sib_id)
        for m in range(1, chans):
            src = (n + chans - m) % chans
            for q in range(clips):
                arrive(slab(src, 1 - core, (z + clips - q) % clips), ("ws", m, q))
        keep_w.wait()

    tap_row(0)
    tap_row(1)
    reduce1(0)
    tap_row(2)
    bias_sum()
    reduce1(1)
    halos()
    reduce2(0)
    reduce1(2)
    weights()
    conv(0)
    reduce2(1)
    gather1(0)
    conv(1)
    reduce2(2)
    gather1(1)
    conv(2)
    gather2(0)
    gather1(2)
    back(0)
    gather2(1)
    cross(0)
    back(1)
    gather2(2)
    cross(1)
    back(2)
    cross(2)
    for q in range(1, clips):
        arrive(dgot.at[q], ("d", q))
    sums = dbs[...]
    for q in range(1, clips):
        sums = sums + dgot[q]
    db_ref[...] = sums[:1] * scale
    for a in range(3):
        finish(a)
    for copy in started:
        copy.wait_send()


def emit(*refs):
    sources, places, sems = refs[:4], refs[4:8], refs[8]
    copies = [pltpu.make_async_copy(src, dst, sems.at[i]) for i, (src, dst) in enumerate(zip(sources, places))]
    for copy in copies:
        copy.start()
    for copy in copies:
        copy.wait()


VM = pl.BlockSpec(memory_space=pltpu.VMEM)


def local(frames, weight, bias, cotangent):
    channels, frame_count, cells = frames.shape
    clips, bands, chans = (lax.axis_size(a) for a in ("clip", "band", "chan"))
    group = bands * chans
    assert frame_count == 1 and cells % W == 0 and clips == 4
    total = cells * group
    scale = 1.0 / math.sqrt(frame_count * clips * total)
    rows_i, rows_o = channels // bands, channels // chans
    x = frames.reshape(channels, cells)
    g = cotangent.reshape(channels, cells)
    wt = jnp.transpose(weight, (1, 2, 0, 3)).reshape(9, rows_o, channels)
    half = rows_o // 2
    width = bands // 2
    copies = (chans - 1) * (1 + clips - 1 + clips) + 2 * width * chans + group + bands * chans + 4 + 12 + clips + 9 * (2 * width) + 8
    limit = (24 << 20) + (total + 2 * W) * 4 * rows_i * 2 + rows_o * total * 2 + rows_o * channels * 72
    shape = jax.ShapeDtypeStruct
    grad, db, outputs, back = pl.pallas_call(
        functools.partial(kernel, (clips, bands, chans, rows_o, rows_i, cells, channels, scale)),
        out_shape=(
            shape((9, rows_o, channels), F32),
            shape((1, rows_o), F32),
            shape((channels, cells), BF16),
            shape((channels, cells), BF16),
        ),
        in_specs=[VM] * 4,
        out_specs=(VM,) * 4,
        scratch_shapes=[
            pltpu.VMEM((total, rows_i), BF16),
            pltpu.VMEM((rows_o, total), BF16),
            pltpu.VMEM((total + 2 * W, 3 * rows_i), BF16),
            pltpu.VMEM((cells + 2 * W, 3 * channels), BF16),
            pltpu.VMEM((cells + 2 * W, 3 * channels), BF16),
            pltpu.VMEM((9, channels, channels), BF16),
            pltpu.VMEM((max(channels, cells), max(channels, cells)), F32),
            pltpu.VMEM((9, rows_o, rows_i), F32),
            pltpu.VMEM((9, half, rows_i), F32),
            pltpu.VMEM((9, half // 2, rows_i), F32),
            pltpu.VMEM((8, rows_o), F32),
            pltpu.VMEM((clips, 8, rows_o), F32),
            pltpu.VMEM((2, W, channels), BF16),
            pltpu.VMEM((2, W, channels), BF16),
            pltpu.VMEM((cells, channels), BF16),
            pltpu.VMEM((cells, channels), BF16),
            pltpu.SemaphoreType.DMA((2, copies)),
            pltpu.SemaphoreType.DMA((3,)),
        ],
        compiler_params=pltpu.CompilerParams(collective_id=0, has_side_effects=True, vmem_limit_bytes=min(67000000, limit)),
    )(x, g, wt, bias[None, :])
    results = (grad, db, outputs, back)
    grad, db, outputs, back = pl.pallas_call(
        emit,
        out_shape=tuple(shape(r.shape, r.dtype) for r in results),
        in_specs=[VM] * 4,
        out_specs=(pl.BlockSpec(memory_space=pl.ANY),) * 4,
        scratch_shapes=[pltpu.SemaphoreType.DMA((4,))],
        compiler_params=pltpu.CompilerParams(vmem_limit_bytes=16 << 20),
    )(*results)
    outputs = outputs.reshape(frames.shape)
    grad_frames = back.reshape(frames.shape)
    grad_weight = jnp.transpose(grad.reshape(3, 3, rows_o, channels), (2, 0, 1, 3))
    return outputs, grad_frames, grad_weight, db[0]


def solution(mesh):
    cells = P(None, "clip", ("band", "chan"))
    taps = P("chan", None, None, None)
    return jax.shard_map(
        local, mesh=mesh, in_specs=(cells, taps, P(), cells), out_specs=(cells, cells, taps, P("chan")), check_vma=False
    )
```

```python
import functools
import math

import jax
import jax.numpy as jnp
from jax import lax
from jax.experimental import pallas as pl
from jax.experimental.pallas import tpu as pltpu
from jax.sharding import PartitionSpec as P

W = 160
MESH = pl.DeviceIdType.MESH
F32 = jnp.float32
BF16 = jnp.bfloat16


def ds(start, size):
    return pl.ds(pl.multiple_of(start, size), size)


def remote(src, dst, send, recv, device):
    return pltpu.make_async_remote_copy(
        src_ref=src, dst_ref=dst, send_sem=send, recv_sem=recv, device_id=device, device_id_type=MESH
    )


def sides(rows):
    wide = rows.astype(F32)
    at = lax.broadcasted_iota(jnp.int32, wide.shape, 0)
    left = jnp.where(at == 0, 0.0, pltpu.roll(wide, 1, 0)).astype(BF16)
    right = jnp.where(at == W - 1, 0.0, pltpu.roll(wide, W - 1, 0)).astype(BF16)
    return left, rows, right


def kernel(
    dims, x_in, g_in, w_ref, bias_in, o_ref, db_ref, out_ref, back_ref,
    xs, gs, dx, xe, ge, kern, acc, share, got1, got2, dbs, dgot, hx, hg, xt_ref, gt_ref, x_ref, g_ref, bias_ref, sems, regs,
):
    clips, bands, chans, rows_o, rows_i, cells, channels, scale = dims
    group = bands * chans
    half = rows_o // 2
    lanes = channels // clips
    width = bands // 2
    units = cells // W
    total = cells * group
    z, b, n = lax.axis_index("clip"), lax.axis_index("band"), lax.axis_index("chan")
    me = b * chans + n
    core = b % 2
    sib = b + 1 - 2 * core
    sib_id = {"band": sib}
    nxt, prv = (me + 1) % group, (me + group - 1) % group
    nxt_id = {"band": nxt // chans, "chan": nxt % chans}
    prv_id = {"band": prv // chans, "chan": prv % chans}
    z0 = z % 2
    inner = (z + 1) // 2 == 1
    near, middle = {"clip": z + 1 - 2 * z0}, {"clip": clips - 1 - z}

    loads = [
        pltpu.make_async_copy(src, dst, regs.at[3 + i])
        for i, (src, dst) in enumerate(((x_in, x_ref), (g_in, g_ref), (bias_in, bias_ref)))
    ]
    for load in loads:
        load.start()
    barrier = pltpu.get_barrier_semaphore()
    targets = [{"clip": (z + k) % clips} for k in range(1, clips)]
    for k in range(1, group):
        to = (me + k) % group
        targets.append({"band": to // chans, "chan": to % chans})
    for target in targets:
        pl.semaphore_signal(barrier, inc=1, device_id=target, device_id_type=MESH)

    def turn(src, dst):
        @pl.loop(0, cells // 128)
        def _(t):
            dst[ds(t * 128, 128), :] = src[:, ds(t * 128, 128)].astype(F32).T.astype(BF16)

    loads[0].wait()
    turn(x_ref, xt_ref)
    loads[1].wait()
    loads[2].wait()
    pl.semaphore_wait(barrier, len(targets))

    started = []
    names = {}

    def pair(key):
        if key not in names:
            names[key] = len(names)
        return sems.at[0, names[key]], sems.at[1, names[key]]

    def send(src, dst, key, device):
        s, r = pair(key)
        copy = remote(src, dst, s, r, device)
        copy.start()
        started.append(copy)

    def arrive(dst, key):
        s, r = pair(key)
        remote(dst, dst, s, r, sib_id).wait_recv()

    def slab(src_n, part, zz):
        return kern.at[:, ds((2 * src_n + part) * half, half), ds(zz * lanes, lanes)]

    keep_w = pltpu.make_async_copy(w_ref, kern.at[:, ds(n * rows_o, rows_o), :], regs.at[0])
    keep_x = pltpu.make_async_copy(xt_ref.at[:, ds(b * rows_i, rows_i)], xs.at[ds(me * cells, cells), :], regs.at[1])
    keep_g = pltpu.make_async_copy(g_ref.at[ds(n * rows_o, rows_o), :], gs.at[:, ds(me * cells, cells)], regs.at[2])

    def x_place(src_b, src_n):
        return xs.at[ds((src_b * chans + src_n) * cells, cells), :]

    def g_place(src_b, src_n):
        return gs.at[:, ds((src_b * chans + src_n) * cells, cells)]

    for m in range(1, chans):
        send(w_ref.at[:, ds(core * half, half), ds(z * lanes, lanes)], slab(n, core, z), ("w", m), {"chan": (n + m) % chans})
    for d in range(1, bands):
        to_b = (b + d) % bands
        send(xt_ref.at[:, ds(to_b * rows_i, rows_i)], x_place(b, n), ("x", d, 0), {"band": to_b})
    for m in range(1, chans):
        to_n = (n + m) % chans
        send(g_ref.at[ds(to_n * rows_o, rows_o), :], g_place(b, n), ("g", 0, m), {"chan": to_n})
        send(xt_ref.at[:, ds(b * rows_i, rows_i)], x_place(b, n), ("x", 0, m), {"chan": to_n})
    own_g = g_ref.at[ds(n * rows_o, rows_o), :]
    for j in range(1, width):
        send(own_g, g_place(b, n), ("g", j, 0), {"band": (b + 2 * j) % bands})
    send(own_g, g_place(b, n), ("f", 0, 0), sib_id)
    keep_x.start()
    keep_g.start()
    keep_w.start()

    def widen(dst, to, rows, size):
        for t, part in enumerate(sides(rows)):
            dst[ds(to, W), t * size:(t + 1) * size] = part

    def widen_block(src):
        @pl.loop(0, units)
        def _(u):
            at = src * cells + u * W
            widen(dx, at + W, xs[ds(at, W), :], rows_i)

    for m in range(1, chans):
        src = (n + chans - m) % chans
        arrive(slab(src, core, z), ("w", m))
        for q in range(1, clips):
            send(slab(src, core, z), slab(src, core, z), ("wz", m, q), {"clip": (z + q) % clips})
        send(slab(src, core, z), slab(src, core, z), ("ws", m, 0), sib_id)
    for d in range(1, bands):
        place = x_place((b + bands - d) % bands, n)
        arrive(place, ("x", d, 0))
        for m in range(1, chans):
            send(place, place, ("x", d, m), {"chan": (n + m) % chans})
    for m in range(1, chans):
        place = g_place(b, (n + chans - m) % chans)
        arrive(place, ("g", 0, m))
        for j in range(1, width):
            send(place, place, ("g", j, m), {"band": (b + 2 * j) % bands})
        send(place, place, ("f", 0, m), sib_id)
    for j in range(1, width):
        place = g_place((b + bands - 2 * j) % bands, n)
        arrive(place, ("g", j, 0))
        send(place, place, ("f", j, 0), sib_id)

    turn(g_ref, gt_ref)
    dx[pl.ds(0, W), :] = jnp.zeros((W, 3 * rows_i), BF16)
    dx[pl.ds(total + W, W), :] = jnp.zeros((W, 3 * rows_i), BF16)

    @pl.loop(0, units)
    def _(u):
        widen(xe, (u + 1) * W, xt_ref[ds(u * W, W), :], channels)
        widen(ge, (u + 1) * W, gt_ref[ds(u * W, W), :], channels)

    keep_x.wait()
    widen_block(me)
    for d in range(1, bands):
        widen_block(((b + bands - d) % bands) * chans + n)
    for m in range(1, chans):
        src_n = (n + chans - m) % chans
        arrive(x_place(b, src_n), ("x", 0, m))
        widen_block(b * chans + src_n)
    for j in range(1, width):
        for m in range(1, chans):
            place = g_place((b + bands - 2 * j) % bands, (n + chans - m) % chans)
            arrive(place, ("g", j, m))
            send(place, place, ("f", j, m), sib_id)
    for d in range(1, bands):
        for m in range(1, chans):
            src_b, src_n = (b + bands - d) % bands, (n + chans - m) % chans
            arrive(x_place(src_b, src_n), ("x", d, m))
            widen_block(src_b * chans + src_n)
    send(xt_ref.at[pl.ds(cells - W, W), :], hx.at[0], ("hx", 0), nxt_id)
    send(gt_ref.at[pl.ds(cells - W, W), :], hg.at[0], ("hg", 0), nxt_id)
    send(xt_ref.at[pl.ds(0, W), :], hx.at[1], ("hx", 1), prv_id)
    send(gt_ref.at[pl.ds(0, W), :], hg.at[1], ("hg", 1), prv_id)
    for j in range(width):
        for m in range(chans):
            arrive(g_place((sib + bands - 2 * j) % bands, (n + chans - m) % chans), ("f", j, m))
    keep_g.wait()

    block = 2 * cells

    def tap_row(a):
        acc2 = acc.at[pl.ds(0, rows_o), pl.ds(0, 3 * rows_i)]
        acc2[...] = jnp.zeros((rows_o, 3 * rows_i), F32)

        @pl.loop(0, group // 2)
        def _(k):
            rows = pl.ds(pl.multiple_of(k * block + a * W, 32), block)
            acc2[...] += jnp.dot(gs[:, ds(k * block, block)], dx[rows, :], preferred_element_type=F32)

        for t in range(3):
            share[3 * a + t] = acc2[:, t * rows_i:(t + 1) * rows_i] * scale

    side = z // 2

    def spot(t, part, bb):
        return o_ref.at[t, ds(part * half, half), ds(bb * rows_i, rows_i)]

    def spread(t, part, step):
        place = spot(t, part, b)
        for j in range(1, width):
            send(place, place, ("xo", t, step, j), {"band": (b + 2 * j) % bands})
        send(place, place, ("c", t, step, 0), sib_id)

    def give(t):
        send(share.at[t], got1.at[t], ("r1", t), near)

    def take(t):
        arrive(got1.at[t], ("r1", t))
        share[t] += got1[t]
        send(share.at[t, ds((1 - side) * half, half), :], got2.at[t], ("r2", t), middle)

    def settle(t):
        arrive(got2.at[t], ("r2", t))
        o_ref[t, ds(side * half, half), ds(b * rows_i, rows_i)] = share[t, ds(side * half, half), :] + got2[t]
        place = spot(t, side, b)
        send(place, place, ("a1", t), middle)
        send(place, place, ("a2", t, 0), near)
        spread(t, side, 0)

    def share_back(t):
        place = spot(t, 1 - side, b)
        arrive(place, ("a1", t))
        send(place, place, ("a2", t, 1), near)
        spread(t, 1 - side, 1)

    def receive(t):
        for step, part in enumerate((side, 1 - side)):
            arrive(spot(t, part, b), ("a2", t, step))
            spread(t, part, step)

    def cross(t):
        for step, part in enumerate((side, 1 - side)):
            for j in range(1, width):
                place = spot(t, part, (b + bands - 2 * j) % bands)
                arrive(place, ("xo", t, step, j))
                send(place, place, ("c", t, step, j), sib_id)

    def finish(t):
        for step, part in enumerate((side, 1 - side)):
            for j in range(width):
                arrive(spot(t, part, (sib + bands - 2 * j) % bands), ("c", t, step, j))

    def conv(a):
        @pl.loop(0, channels // 256)
        def _(t):
            rows = ds(t * 256, 256)
            if a == 0:
                column = jnp.broadcast_to(bias_ref[:, rows], (8, 256)).T[:, :1]
                part = jnp.zeros((256, cells), F32) + column
            else:
                part = acc[rows, :]
            for s in range(3):
                part += lax.dot_general(
                    kern[3 * a + s, rows, :], xe[a * W:a * W + cells, s * channels:(s + 1) * channels],
                    (((1,), (1,)), ((), ())), preferred_element_type=F32,
                )
            if a == 2:
                out_ref[rows, :] = part.astype(BF16)
            else:
                acc[rows, :] = part

    half_cells = cells // 2

    def back(a):
        @pl.loop(0, 2)
        def _(t):
            rows = ds(t * half_cells, half_cells)
            c = 2 - a
            part = jnp.zeros((half_cells, channels), F32)
            if a:
                part = acc[ds(t * half_cells, half_cells), pl.ds(0, channels)]
            for s in range(3):
                part += jnp.dot(
                    ge[pl.ds(pl.multiple_of(c * W + t * half_cells, 32), half_cells), (2 - s) * channels:(3 - s) * channels],
                    kern[3 * a + s], preferred_element_type=F32,
                )
            acc[rows, pl.ds(0, channels)] = part

        if a == 2:
            @pl.loop(0, cells // 128)
            def _(t):
                back_ref[:, ds(t * 128, 128)] = acc[ds(t * 128, 128), pl.ds(0, channels)].T.astype(BF16)

    def bias_sum():
        ones = jnp.ones((8, block), BF16)
        dbs[...] = jnp.zeros((8, rows_o), F32)

        @pl.loop(0, group // 2)
        def _(k):
            dbs[...] += lax.dot_general(
                ones, gs[:, ds(k * block, block)], (((1,), (1,)), ((), ())), preferred_element_type=F32
            )

        for q in range(1, clips):
            send(dbs, dgot.at[q], ("d", q), {"clip": (z + q) % clips})

    def halos():
        for h in range(2):
            arrive(hx.at[h], ("hx", h))
            arrive(hg.at[h], ("hg", h))
            edge = me == (0 if h == 0 else group - 1)
            for src, dst in ((hx, xe), (hg, ge)):
                rows = src[h]
                rows = jnp.where(edge, jnp.zeros_like(rows), rows)
                for t, part in enumerate(sides(rows)):
                    dst[pl.ds(h * (cells + W), W), t * channels:(t + 1) * channels] = part

    def weights():
        for m in range(1, chans):
            src = (n + chans - m) % chans
            for q in range(1, clips):
                zz = (z + clips - q) % clips
                arrive(slab(src, core, zz), ("wz", m, q))
                send(slab(src, core, zz), slab(src, core, zz), ("ws", m, q), sib_id)
        for m in range(1, chans):
            src = (n + chans - m) % chans
            for q in range(clips):
                arrive(slab(src, 1 - core, (z + clips - q) % clips), ("ws", m, q))
        keep_w.wait()

    def matmuls():
        yield halos()
        yield weights()
        for a in range(3):
            yield conv(a)
        for a in range(3):
            yield back(a)

    gathered = list(started)

    def second_half(role):
        started.clear()
        work = matmuls()
        for a in range(3):
            tap_row(a)
            if not role:
                for t in range(3 * a, 3 * a + 3):
                    give(t)
        bias_sum()
        if role:
            for t in range(13):
                for step, lag in ((take, 0), (settle, 1), (share_back, 2), (cross, 4)):
                    if 0 <= t - lag < 9:
                        step(t - lag)
                next(work, None)
        else:
            for _ in range(4):
                next(work)
            for t in range(11):
                for step, lag in ((receive, 0), (cross, 2)):
                    if 0 <= t - lag < 9:
                        step(t - lag)
                next(work, None)
        for q in range(1, clips):
            arrive(dgot.at[q], ("d", q))
        sums = dbs[...]
        for q in range(1, clips):
            sums = sums + dgot[q]
        db_ref[...] = sums[:1] * scale
        for t in range(9):
            finish(t)
        for copy in started:
            copy.wait_send()

    @pl.when(inner)
    def _():
        second_half(True)

    @pl.when(jnp.logical_not(inner))
    def _():
        second_half(False)

    for copy in gathered:
        copy.wait_send()


def emit(*refs):
    sources, places, sems = refs[:4], refs[4:8], refs[8]
    copies = [pltpu.make_async_copy(src, dst, sems.at[i]) for i, (src, dst) in enumerate(zip(sources, places))]
    for copy in copies:
        copy.start()
    for copy in copies:
        copy.wait()


VM = pl.BlockSpec(memory_space=pltpu.VMEM)


def local(frames, weight, bias, cotangent):
    channels, frame_count, cells = frames.shape
    clips, bands, chans = (lax.axis_size(a) for a in ("clip", "band", "chan"))
    group = bands * chans
    assert frame_count == 1 and cells % W == 0 and clips == 4
    total = cells * group
    scale = 1.0 / math.sqrt(frame_count * clips * total)
    rows_i, rows_o = channels // bands, channels // chans
    x = frames.reshape(channels, cells)
    g = cotangent.reshape(channels, cells)
    wt = jnp.transpose(weight, (1, 2, 0, 3)).reshape(9, rows_o, channels)
    half = rows_o // 2
    width = bands // 2
    copies = (chans - 1) * (1 + clips - 1 + clips) + 2 * width * chans + group + bands * chans + 4 + clips + 9 * (5 + 4 * width) + 8
    limit = (24 << 20) + (total + 2 * W) * 4 * rows_i * 2 + rows_o * total * 2 + rows_o * channels * 72
    shape = jax.ShapeDtypeStruct
    grad, db, outputs, back = pl.pallas_call(
        functools.partial(kernel, (clips, bands, chans, rows_o, rows_i, cells, channels, scale)),
        out_shape=(
            shape((9, rows_o, channels), F32),
            shape((1, rows_o), F32),
            shape((channels, cells), BF16),
            shape((channels, cells), BF16),
        ),
        in_specs=[pl.BlockSpec(memory_space=pltpu.HBM)] * 4,
        out_specs=(VM,) * 4,
        scratch_shapes=[
            pltpu.VMEM((total, rows_i), BF16),
            pltpu.VMEM((rows_o, total), BF16),
            pltpu.VMEM((total + 2 * W, 3 * rows_i), BF16),
            pltpu.VMEM((cells + 2 * W, 3 * channels), BF16),
            pltpu.VMEM((cells + 2 * W, 3 * channels), BF16),
            pltpu.VMEM((9, channels, channels), BF16),
            pltpu.VMEM((max(channels, cells), max(channels, cells)), F32),
            pltpu.VMEM((9, rows_o, rows_i), F32),
            pltpu.VMEM((9, rows_o, rows_i), F32),
            pltpu.VMEM((9, half, rows_i), F32),
            pltpu.VMEM((8, rows_o), F32),
            pltpu.VMEM((clips, 8, rows_o), F32),
            pltpu.VMEM((2, W, channels), BF16),
            pltpu.VMEM((2, W, channels), BF16),
            pltpu.VMEM((cells, channels), BF16),
            pltpu.VMEM((cells, channels), BF16),
            pltpu.VMEM((channels, cells), BF16),
            pltpu.VMEM((channels, cells), BF16),
            pltpu.VMEM((1, channels), F32),
            pltpu.SemaphoreType.DMA((2, copies)),
            pltpu.SemaphoreType.DMA((6,)),
        ],
        compiler_params=pltpu.CompilerParams(collective_id=0, has_side_effects=True, vmem_limit_bytes=min(67000000, limit)),
    )(x, g, wt, bias[None, :])
    results = (grad, db, outputs, back)
    grad, db, outputs, back = pl.pallas_call(
        emit,
        out_shape=tuple(shape(r.shape, r.dtype) for r in results),
        in_specs=[VM] * 4,
        out_specs=(pl.BlockSpec(memory_space=pl.ANY),) * 4,
        scratch_shapes=[pltpu.SemaphoreType.DMA((4,))],
        compiler_params=pltpu.CompilerParams(vmem_limit_bytes=16 << 20),
    )(*results)
    outputs = outputs.reshape(frames.shape)
    grad_frames = back.reshape(frames.shape)
    grad_weight = jnp.transpose(grad.reshape(3, 3, rows_o, channels), (2, 0, 1, 3))
    return outputs, grad_frames, grad_weight, db[0]


def solution(mesh):
    cells = P(None, "clip", ("band", "chan"))
    taps = P("chan", None, None, None)
    return jax.shard_map(
        local, mesh=mesh, in_specs=(cells, taps, P(), cells), out_specs=(cells, cells, taps, P("chan")), check_vma=False
    )
```

```python
import functools
import math

import jax
import jax.numpy as jnp
from jax import lax
from jax.experimental import pallas as pl
from jax.experimental.pallas import tpu as pltpu
from jax.sharding import PartitionSpec as P

W = 160
MESH = pl.DeviceIdType.MESH
F32 = jnp.float32
BF16 = jnp.bfloat16


def ds(start, size):
    return pl.ds(pl.multiple_of(start, size), size)


def remote(src, dst, send, recv, device):
    return pltpu.make_async_remote_copy(
        src_ref=src, dst_ref=dst, send_sem=send, recv_sem=recv, device_id=device, device_id_type=MESH
    )


def sides(rows):
    wide = rows.astype(F32)
    at = lax.broadcasted_iota(jnp.int32, wide.shape, 0)
    left = jnp.where(at == 0, 0.0, pltpu.roll(wide, 1, 0)).astype(BF16)
    right = jnp.where(at == W - 1, 0.0, pltpu.roll(wide, W - 1, 0)).astype(BF16)
    return left, rows, right


def kernel(
    dims, x_in, g_in, w_ref, bias_in, o_ref, db_ref, out_ref, back_ref,
    xs, gs, dx, xe, ge, kern, acc, share, got1, got2, dbs, dgot, hx, hg, xt_ref, gt_ref, x_ref, g_ref, bias_ref, sems, regs,
):
    clips, bands, chans, rows_o, rows_i, cells, channels, scale = dims
    group = bands * chans
    half = rows_o // 2
    lanes = channels // clips
    width = bands // 2
    units = cells // W
    total = cells * group
    z, b, n = lax.axis_index("clip"), lax.axis_index("band"), lax.axis_index("chan")
    me = b * chans + n
    core = b % 2
    sib = b + 1 - 2 * core
    sib_id = {"band": sib}
    nxt, prv = (me + 1) % group, (me + group - 1) % group
    nxt_id = {"band": nxt // chans, "chan": nxt % chans}
    prv_id = {"band": prv // chans, "chan": prv % chans}
    z0 = z % 2
    inner = (z + 1) // 2 == 1
    near, middle = {"clip": z + 1 - 2 * z0}, {"clip": clips - 1 - z}

    loads = [
        pltpu.make_async_copy(src, dst, regs.at[3 + i])
        for i, (src, dst) in enumerate(((x_in, x_ref), (g_in, g_ref), (bias_in, bias_ref)))
    ]
    for load in loads:
        load.start()
    barrier = pltpu.get_barrier_semaphore()
    targets = [{"clip": (z + k) % clips} for k in range(1, clips)]
    for k in range(1, group):
        to = (me + k) % group
        targets.append({"band": to // chans, "chan": to % chans})
    for target in targets:
        pl.semaphore_signal(barrier, inc=1, device_id=target, device_id_type=MESH)

    def turn(src, dst):
        @pl.loop(0, cells // 128)
        def _(t):
            dst[ds(t * 128, 128), :] = src[:, ds(t * 128, 128)].astype(F32).T.astype(BF16)

    loads[0].wait()
    turn(x_ref, xt_ref)
    loads[1].wait()
    loads[2].wait()
    pl.semaphore_wait(barrier, len(targets))

    started = []
    names = {}

    def pair(key):
        if key not in names:
            names[key] = len(names)
        return sems.at[0, names[key]], sems.at[1, names[key]]

    def send(src, dst, key, device):
        s, r = pair(key)
        copy = remote(src, dst, s, r, device)
        copy.start()
        started.append(copy)

    def arrive(dst, key):
        s, r = pair(key)
        remote(dst, dst, s, r, sib_id).wait_recv()

    def slab(src_n, part, zz):
        return kern.at[:, ds((2 * src_n + part) * half, half), ds(zz * lanes, lanes)]

    keep_w = pltpu.make_async_copy(w_ref, kern.at[:, ds(n * rows_o, rows_o), :], regs.at[0])
    keep_x = pltpu.make_async_copy(xt_ref.at[:, ds(b * rows_i, rows_i)], xs.at[ds(me * cells, cells), :], regs.at[1])
    keep_g = pltpu.make_async_copy(g_ref.at[ds(n * rows_o, rows_o), :], gs.at[:, ds(me * cells, cells)], regs.at[2])

    def x_place(src_b, src_n):
        return xs.at[ds((src_b * chans + src_n) * cells, cells), :]

    def g_place(src_b, src_n):
        return gs.at[:, ds((src_b * chans + src_n) * cells, cells)]

    for m in range(1, chans):
        send(w_ref.at[:, ds(core * half, half), ds(z * lanes, lanes)], slab(n, core, z), ("w", m), {"chan": (n + m) % chans})
    for d in range(1, bands):
        to_b = (b + d) % bands
        send(xt_ref.at[:, ds(to_b * rows_i, rows_i)], x_place(b, n), ("x", d, 0), {"band": to_b})
    for m in range(1, chans):
        to_n = (n + m) % chans
        send(g_ref.at[ds(to_n * rows_o, rows_o), :], g_place(b, n), ("g", 0, m), {"chan": to_n})
        send(xt_ref.at[:, ds(b * rows_i, rows_i)], x_place(b, n), ("x", 0, m), {"chan": to_n})
    own_g = g_ref.at[ds(n * rows_o, rows_o), :]
    for j in range(1, width):
        send(own_g, g_place(b, n), ("g", j, 0), {"band": (b + 2 * j) % bands})
    send(own_g, g_place(b, n), ("f", 0, 0), sib_id)
    keep_x.start()
    keep_g.start()
    keep_w.start()

    def widen(dst, to, rows, size):
        for t, part in enumerate(sides(rows)):
            dst[ds(to, W), t * size:(t + 1) * size] = part

    def widen_block(src):
        @pl.loop(0, units)
        def _(u):
            at = src * cells + u * W
            widen(dx, at + W, xs[ds(at, W), :], rows_i)

    for m in range(1, chans):
        src = (n + chans - m) % chans
        arrive(slab(src, core, z), ("w", m))
        for q in range(1, clips):
            send(slab(src, core, z), slab(src, core, z), ("wz", m, q), {"clip": (z + q) % clips})
        send(slab(src, core, z), slab(src, core, z), ("ws", m, 0), sib_id)
    for d in range(1, bands):
        place = x_place((b + bands - d) % bands, n)
        arrive(place, ("x", d, 0))
        for m in range(1, chans):
            send(place, place, ("x", d, m), {"chan": (n + m) % chans})
    for m in range(1, chans):
        place = g_place(b, (n + chans - m) % chans)
        arrive(place, ("g", 0, m))
        for j in range(1, width):
            send(place, place, ("g", j, m), {"band": (b + 2 * j) % bands})
        send(place, place, ("f", 0, m), sib_id)
    for j in range(1, width):
        place = g_place((b + bands - 2 * j) % bands, n)
        arrive(place, ("g", j, 0))
        send(place, place, ("f", j, 0), sib_id)

    turn(g_ref, gt_ref)
    dx[pl.ds(0, W), :] = jnp.zeros((W, 3 * rows_i), BF16)
    dx[pl.ds(total + W, W), :] = jnp.zeros((W, 3 * rows_i), BF16)

    @pl.loop(0, units)
    def _(u):
        widen(xe, (u + 1) * W, xt_ref[ds(u * W, W), :], channels)
        widen(ge, (u + 1) * W, gt_ref[ds(u * W, W), :], channels)

    keep_x.wait()
    widen_block(me)
    for d in range(1, bands):
        widen_block(((b + bands - d) % bands) * chans + n)
    for m in range(1, chans):
        src_n = (n + chans - m) % chans
        arrive(x_place(b, src_n), ("x", 0, m))
        widen_block(b * chans + src_n)
    for j in range(1, width):
        for m in range(1, chans):
            place = g_place((b + bands - 2 * j) % bands, (n + chans - m) % chans)
            arrive(place, ("g", j, m))
            send(place, place, ("f", j, m), sib_id)
    for d in range(1, bands):
        for m in range(1, chans):
            src_b, src_n = (b + bands - d) % bands, (n + chans - m) % chans
            arrive(x_place(src_b, src_n), ("x", d, m))
            widen_block(src_b * chans + src_n)
    send(xt_ref.at[pl.ds(cells - W, W), :], hx.at[0], ("hx", 0), nxt_id)
    send(gt_ref.at[pl.ds(cells - W, W), :], hg.at[0], ("hg", 0), nxt_id)
    send(xt_ref.at[pl.ds(0, W), :], hx.at[1], ("hx", 1), prv_id)
    send(gt_ref.at[pl.ds(0, W), :], hg.at[1], ("hg", 1), prv_id)
    for j in range(width):
        for m in range(chans):
            arrive(g_place((sib + bands - 2 * j) % bands, (n + chans - m) % chans), ("f", j, m))
    keep_g.wait()

    block = 2 * cells

    def tap_row(a):
        acc2 = acc.at[pl.ds(0, rows_o), pl.ds(0, 3 * rows_i)]
        acc2[...] = jnp.zeros((rows_o, 3 * rows_i), F32)

        @pl.loop(0, group // 2)
        def _(k):
            rows = pl.ds(pl.multiple_of(k * block + a * W, 32), block)
            acc2[...] += jnp.dot(gs[:, ds(k * block, block)], dx[rows, :], preferred_element_type=F32)

        for t in range(3):
            share[3 * a + t] = acc2[:, t * rows_i:(t + 1) * rows_i] * scale

    side = z // 2

    def spot(t, part, bb):
        return o_ref.at[t, ds(part * half, half), ds(bb * rows_i, rows_i)]

    def spread(t, part, step):
        place = spot(t, part, b)
        for j in range(1, width):
            send(place, place, ("xo", t, step, j), {"band": (b + 2 * j) % bands})
        send(place, place, ("c", t, step, 0), sib_id)

    def give(t):
        send(share.at[t], got1.at[t], ("r1", t), near)

    def take(t):
        arrive(got1.at[t], ("r1", t))
        share[t] += got1[t]
        send(share.at[t, ds((1 - side) * half, half), :], got2.at[t], ("r2", t), middle)

    def settle(t):
        arrive(got2.at[t], ("r2", t))
        o_ref[t, ds(side * half, half), ds(b * rows_i, rows_i)] = share[t, ds(side * half, half), :] + got2[t]
        place = spot(t, side, b)
        send(place, place, ("a1", t), middle)
        send(place, place, ("a2", t, 0), near)
        spread(t, side, 0)

    def share_back(t):
        place = spot(t, 1 - side, b)
        arrive(place, ("a1", t))
        send(place, place, ("a2", t, 1), near)
        spread(t, 1 - side, 1)

    def receive(t):
        for step, part in enumerate((side, 1 - side)):
            arrive(spot(t, part, b), ("a2", t, step))
            spread(t, part, step)

    def cross(t):
        for step, part in enumerate((side, 1 - side)):
            for j in range(1, width):
                place = spot(t, part, (b + bands - 2 * j) % bands)
                arrive(place, ("xo", t, step, j))
                send(place, place, ("c", t, step, j), sib_id)

    def finish(t):
        for step, part in enumerate((side, 1 - side)):
            for j in range(width):
                arrive(spot(t, part, (sib + bands - 2 * j) % bands), ("c", t, step, j))

    def conv(a):
        @pl.loop(0, channels // 256)
        def _(t):
            rows = ds(t * 256, 256)
            if a == 0:
                column = jnp.broadcast_to(bias_ref[:, rows], (8, 256)).T[:, :1]
                part = jnp.zeros((256, cells), F32) + column
            else:
                part = acc[rows, :]
            for s in range(3):
                part += lax.dot_general(
                    kern[3 * a + s, rows, :], xe[a * W:a * W + cells, s * channels:(s + 1) * channels],
                    (((1,), (1,)), ((), ())), preferred_element_type=F32,
                )
            if a == 2:
                out_ref[rows, :] = part.astype(BF16)
            else:
                acc[rows, :] = part

    half_cells = cells // 2

    def back(a):
        @pl.loop(0, 2)
        def _(t):
            rows = ds(t * half_cells, half_cells)
            c = 2 - a
            part = jnp.zeros((half_cells, channels), F32)
            if a:
                part = acc[ds(t * half_cells, half_cells), pl.ds(0, channels)]
            for s in range(3):
                part += jnp.dot(
                    ge[pl.ds(pl.multiple_of(c * W + t * half_cells, 32), half_cells), (2 - s) * channels:(3 - s) * channels],
                    kern[3 * a + s], preferred_element_type=F32,
                )
            acc[rows, pl.ds(0, channels)] = part

        if a == 2:
            @pl.loop(0, cells // 128)
            def _(t):
                back_ref[:, ds(t * 128, 128)] = acc[ds(t * 128, 128), pl.ds(0, channels)].T.astype(BF16)

    def bias_sum():
        ones = jnp.ones((8, block), BF16)
        dbs[...] = jnp.zeros((8, rows_o), F32)

        @pl.loop(0, group // 2)
        def _(k):
            dbs[...] += lax.dot_general(
                ones, gs[:, ds(k * block, block)], (((1,), (1,)), ((), ())), preferred_element_type=F32
            )

        for q in range(1, clips):
            send(dbs, dgot.at[q], ("d", q), {"clip": (z + q) % clips})

    def halos():
        for h in range(2):
            arrive(hx.at[h], ("hx", h))
            arrive(hg.at[h], ("hg", h))
            edge = me == (0 if h == 0 else group - 1)
            for src, dst in ((hx, xe), (hg, ge)):
                rows = src[h]
                rows = jnp.where(edge, jnp.zeros_like(rows), rows)
                for t, part in enumerate(sides(rows)):
                    dst[pl.ds(h * (cells + W), W), t * channels:(t + 1) * channels] = part

    def weights():
        for m in range(1, chans):
            src = (n + chans - m) % chans
            for q in range(1, clips):
                zz = (z + clips - q) % clips
                arrive(slab(src, core, zz), ("wz", m, q))
                send(slab(src, core, zz), slab(src, core, zz), ("ws", m, q), sib_id)
        for m in range(1, chans):
            src = (n + chans - m) % chans
            for q in range(clips):
                arrive(slab(src, 1 - core, (z + clips - q) % clips), ("ws", m, q))
        keep_w.wait()

    def matmuls():
        yield halos()
        yield weights()
        for a in range(3):
            yield conv(a)
        for a in range(3):
            yield back(a)

    gathered = list(started)

    def second_half(role):
        started.clear()
        work = matmuls()
        for a in range(3):
            tap_row(a)
            if not role:
                for t in range(3 * a, 3 * a + 3):
                    give(t)
        bias_sum()
        if role:
            for t in range(13):
                for step, lag in ((take, 0), (settle, 1), (share_back, 2), (cross, 4)):
                    if 0 <= t - lag < 9:
                        step(t - lag)
                if t >= 3:
                    next(work, None)
        else:
            for t in range(11):
                for step, lag in ((receive, 0), (cross, 2)):
                    if 0 <= t - lag < 9:
                        step(t - lag)
                if t >= 2:
                    next(work, None)
        for _ in work:
            pass
        for q in range(1, clips):
            arrive(dgot.at[q], ("d", q))
        sums = dbs[...]
        for q in range(1, clips):
            sums = sums + dgot[q]
        db_ref[...] = sums[:1] * scale
        for t in range(9):
            finish(t)
        for copy in started:
            copy.wait_send()

    @pl.when(inner)
    def _():
        second_half(True)

    @pl.when(jnp.logical_not(inner))
    def _():
        second_half(False)

    for copy in gathered:
        copy.wait_send()


def emit(*refs):
    sources, places, sems = refs[:4], refs[4:8], refs[8]
    copies = [pltpu.make_async_copy(src, dst, sems.at[i]) for i, (src, dst) in enumerate(zip(sources, places))]
    for copy in copies:
        copy.start()
    for copy in copies:
        copy.wait()


VM = pl.BlockSpec(memory_space=pltpu.VMEM)


def local(frames, weight, bias, cotangent):
    channels, frame_count, cells = frames.shape
    clips, bands, chans = (lax.axis_size(a) for a in ("clip", "band", "chan"))
    group = bands * chans
    assert frame_count == 1 and cells % W == 0 and clips == 4
    total = cells * group
    scale = 1.0 / math.sqrt(frame_count * clips * total)
    rows_i, rows_o = channels // bands, channels // chans
    x = frames.reshape(channels, cells)
    g = cotangent.reshape(channels, cells)
    wt = jnp.transpose(weight, (1, 2, 0, 3)).reshape(9, rows_o, channels)
    half = rows_o // 2
    width = bands // 2
    copies = (chans - 1) * (1 + clips - 1 + clips) + 2 * width * chans + group + bands * chans + 4 + clips + 9 * (5 + 4 * width) + 8
    limit = (24 << 20) + (total + 2 * W) * 4 * rows_i * 2 + rows_o * total * 2 + rows_o * channels * 72
    shape = jax.ShapeDtypeStruct
    grad, db, outputs, back = pl.pallas_call(
        functools.partial(kernel, (clips, bands, chans, rows_o, rows_i, cells, channels, scale)),
        out_shape=(
            shape((9, rows_o, channels), F32),
            shape((1, rows_o), F32),
            shape((channels, cells), BF16),
            shape((channels, cells), BF16),
        ),
        in_specs=[pl.BlockSpec(memory_space=pltpu.HBM)] * 4,
        out_specs=(VM,) * 4,
        scratch_shapes=[
            pltpu.VMEM((total, rows_i), BF16),
            pltpu.VMEM((rows_o, total), BF16),
            pltpu.VMEM((total + 2 * W, 3 * rows_i), BF16),
            pltpu.VMEM((cells + 2 * W, 3 * channels), BF16),
            pltpu.VMEM((cells + 2 * W, 3 * channels), BF16),
            pltpu.VMEM((9, channels, channels), BF16),
            pltpu.VMEM((max(channels, cells), max(channels, cells)), F32),
            pltpu.VMEM((9, rows_o, rows_i), F32),
            pltpu.VMEM((9, rows_o, rows_i), F32),
            pltpu.VMEM((9, half, rows_i), F32),
            pltpu.VMEM((8, rows_o), F32),
            pltpu.VMEM((clips, 8, rows_o), F32),
            pltpu.VMEM((2, W, channels), BF16),
            pltpu.VMEM((2, W, channels), BF16),
            pltpu.VMEM((cells, channels), BF16),
            pltpu.VMEM((cells, channels), BF16),
            pltpu.VMEM((channels, cells), BF16),
            pltpu.VMEM((channels, cells), BF16),
            pltpu.VMEM((1, channels), F32),
            pltpu.SemaphoreType.DMA((2, copies)),
            pltpu.SemaphoreType.DMA((6,)),
        ],
        compiler_params=pltpu.CompilerParams(collective_id=0, has_side_effects=True, vmem_limit_bytes=min(67000000, limit)),
    )(x, g, wt, bias[None, :])
    results = (grad, db, outputs, back)
    grad, db, outputs, back = pl.pallas_call(
        emit,
        out_shape=tuple(shape(r.shape, r.dtype) for r in results),
        in_specs=[VM] * 4,
        out_specs=(pl.BlockSpec(memory_space=pl.ANY),) * 4,
        scratch_shapes=[pltpu.SemaphoreType.DMA((4,))],
        compiler_params=pltpu.CompilerParams(vmem_limit_bytes=16 << 20),
    )(*results)
    outputs = outputs.reshape(frames.shape)
    grad_frames = back.reshape(frames.shape)
    grad_weight = jnp.transpose(grad.reshape(3, 3, rows_o, channels), (2, 0, 1, 3))
    return outputs, grad_frames, grad_weight, db[0]


def solution(mesh):
    cells = P(None, "clip", ("band", "chan"))
    taps = P("chan", None, None, None)
    return jax.shard_map(
        local, mesh=mesh, in_specs=(cells, taps, P(), cells), out_specs=(cells, cells, taps, P("chan")), check_vma=False
    )
```
